256 devices in a mesh: cells: 64 (over x, z, core), cols: 4 (over y).
Axes of the slice: x: 4, y: 4, z: 8, core: 2. Of those that a mesh axis runs over, the one named last changes fastest.
Arguments:
- current: float32 [512, 256, 256], P('cells', 'cols'), may hold values from -6 to 6
- voltage: float32 [512, 256, 256], P('cells', 'cols'), may hold values from -6 to 6
- resistance: float32 [512, 256], P('cells'), may hold values from 0.1 to 1
- elastance: float32 [512, 256], P('cells'), may hold values from 0.1 to 1
- port_gain: float32 [512, 256], P('cells'), may hold values from -6 to 6
- symbols: int32 [3, 256, 256], P(None, 'cells'), may hold values from 0 to 3
- neighbours: int32 [512, 16], P('cells'), may hold values from 0 to 511, as said below
- live_counts: int32 [512], P('cells'), may hold values from 1 to 16, as said below
- membership: int32 [512, 1], P('cells'), may hold values from 0 to 15
- inductance_near: bfloat16 [512, 16, 256, 256], P('cells', None, 'cols'), may hold values from -0.09375 to 0.09375
- source_basis: bfloat16 [512, 64, 256], P('cells'), may hold values from -0.0625 to 0.0625
- target_basis: bfloat16 [512, 64, 256], P('cells'), may hold values from -0.75 to 0.75
- translation: bfloat16 [1024, 1024], replicated, may hold values from -0.1875 to 0.1875
Outputs:
- final_current: float32 [512, 256, 256], P('cells', 'cols')
- final_voltage: float32 [512, 256, 256], P('cells', 'cols')
The draws below stay inside these ranges and needn't reach their ends.
Inputs may be any that keep to these rules, and one draw needn't show every extreme that they name: `neighbours`: entry 0 of block row t is t itself; every entry names a block at most 8 blocks from t. Block row t uses the first live_counts[t] entries of its list. `membership`: every cluster has at least one block.
All inputs are finite; a program needn't handle non-finite values.
Results may differ from the reference program's by a relative error of at most 0.003.
Values may be sent and summed in bfloat16 or wider, within the bound.
A program may use at most 64 MiB of HBM per device.

```python
import math
import jax
import jax.numpy as jnp
from jax import lax

CB = 256
RANK = 64
NEAR = 16
REACH = 8
CLUSTERS = 16
STEPS = 3
SCENARIOS = 256
BLOCKS = 512
LANES = 256


def draw_neighbours(key, part):
    row_keys = jax.random.split(key, BLOCKS)
    offsets_all = jnp.concatenate([-jnp.arange(1, REACH + 1, dtype=jnp.int32), jnp.arange(1, REACH + 1, dtype=jnp.int32)])

    def pick_offsets(row_key):
        return jax.random.permutation(row_key, offsets_all)[:NEAR - 1]
    offsets = jax.vmap(pick_offsets)(row_keys)
    offsets = jnp.concatenate([jnp.zeros((BLOCKS, 1), jnp.int32), offsets], axis=1)
    row_ids = jnp.arange(BLOCKS, dtype=jnp.int32)[:, None]
    targets = row_ids + offsets
    outside = (targets < 0) | (targets >= BLOCKS)
    return jnp.where(outside, row_ids - offsets, targets).astype(jnp.int32)


def draw_live_counts(key, part):
    split_keys = jax.random.split(key, 3)
    counts_drawn = jax.random.randint(split_keys[0], (BLOCKS,), 1, NEAR + 1)
    full_row = jax.random.randint(split_keys[1], (), 0, BLOCKS)
    short_row = (full_row + 1 + jax.random.randint(split_keys[2], (), 0, BLOCKS - 1)) % BLOCKS
    return counts_drawn.at[full_row].set(NEAR).at[short_row].set(1).astype(jnp.int32)


def set_ends(entries, rng, low, high):
    longest = entries.shape.index(max(entries.shape))
    spots = []
    for shift in (0, 1):
        where = [jax.random.randint(jax.random.fold_in(rng, axis), (), 0, length) for axis, length in enumerate(entries.shape)]
        where[longest] = (where[longest] + shift) % entries.shape[longest]
        spots.append(tuple(where))
    return entries.at[spots[0]].set(low).at[spots[1]].set(high)


def level_of(rng, dims, cuts, low, largest):
    factor_of, own = 1.0, jax.random.fold_in(rng, 6)
    for position, parts in cuts:
        heights = jnp.exp(jax.random.uniform(jax.random.fold_in(own, position), (parts,), jnp.float32, low / len(cuts), largest / len(cuts)))
        factor_of = factor_of * jnp.repeat(heights, dims[position] // parts).reshape([-1 if axis == position else 1 for axis in range(len(dims))])
    return factor_of


def different_ones(own_key, rows, number_of, top, lift):
    ranking = jax.random.permutation(jax.random.fold_in(own_key, 1), number_of)
    boost = ranking
    for power in range(3):
        boost = boost * boost // number_of
    boost = boost * lift // number_of
    tickets = jax.random.randint(jax.random.fold_in(own_key, 2), (rows, number_of), 0, 4096) + boost
    holders = jax.random.permutation(jax.random.fold_in(own_key, 3), rows)[jnp.arange(number_of) % rows]
    tickets = jnp.where(jnp.arange(rows)[:, None] == holders[None, :], 1 << 14, tickets)
    priority = tickets * number_of + jnp.arange(number_of)
    return lax.top_k(priority.astype(jnp.int32), top)[1].astype(jnp.int32)


def scatter_about(own_key, dims, width, reach, cuts=(), kind=jnp.bfloat16):
    array = jax.random.normal(own_key, dims, jnp.float32) * width
    if len(cuts) > 0:
        array = level_of(own_key, dims, cuts, -0.22, 0.18) * array
    return jnp.clip(array, min=-reach, max=reach).astype(kind)


def setup_inputs(seed: int = 0) -> dict:
    key_list = jax.random.split(jax.random.key(seed), 14)
    current = scatter_about(key_list[0], (BLOCKS, CB, SCENARIOS), 1.0, 6.0, ((0, 64), (1, 4)), jnp.float32)
    voltage = scatter_about(key_list[1], (BLOCKS, CB, SCENARIOS), 1.0, 6.0, ((0, 64), (1, 4)), jnp.float32)
    resistance = jnp.clip(jnp.exp(math.log(1.0) - 2.3025851 * jax.random.uniform(key_list[2], (BLOCKS, CB), jnp.float32) ** level_of(key_list[2], (BLOCKS, CB), ((0, 64),), -0.2, 0.2)), 0.1, 1.0)
    elastance = jnp.clip(jnp.exp(math.log(1.0) - 2.3025851 * jax.random.uniform(key_list[3], (BLOCKS, CB), jnp.float32) ** level_of(key_list[3], (BLOCKS, CB), ((0, 64),), -0.2, 0.2)), 0.1, 1.0)
    port_gain = scatter_about(key_list[4], (BLOCKS, CB), 1.0, 6.0, ((0, 64),), jnp.float32)
    symbols = set_ends(jax.random.randint(key_list[5], (STEPS, LANES, SCENARIOS), 0, 4), jax.random.fold_in(key_list[5], 1), 0, 3).astype(jnp.int32)
    neighbours = draw_neighbours(jax.random.fold_in(key_list[13], 71), 0)
    live_counts = draw_live_counts(jax.random.fold_in(key_list[13], 71), 0)
    membership = different_ones(key_list[8], BLOCKS, CLUSTERS, 1, 512)
    inductance_near = scatter_about(key_list[9], (BLOCKS, NEAR, CB, CB), (NEAR * CB) ** -0.5, 0.09375, ((0, 64), (2, 4)))
    source_basis = scatter_about(key_list[10], (BLOCKS, RANK, CB), (CB * BLOCKS // CLUSTERS) ** -0.5, 0.0625, ((0, 64),))
    target_basis = scatter_about(key_list[11], (BLOCKS, RANK, CB), RANK ** -0.5, 0.75, ((0, 64),))
    translation = scatter_about(key_list[12], (CLUSTERS * RANK, CLUSTERS * RANK), (CLUSTERS * RANK) ** -0.5, 0.1875)
    return dict(current=current, voltage=voltage, resistance=resistance, elastance=elastance, port_gain=port_gain, symbols=symbols, neighbours=neighbours, live_counts=live_counts, membership=membership, inductance_near=inductance_near, source_basis=source_basis, target_basis=target_basis, translation=translation)


def reference(current, voltage, resistance, elastance, port_gain, symbols, neighbours, live_counts, membership, inductance_near, source_basis, target_basis, translation):
    levels = (2 * symbols - 3).astype(jnp.float32) / 3.0
    member = membership[:, 0]
    entry_index = jnp.arange(NEAR, dtype=jnp.int32)
    translation_wide = translation.astype(jnp.float32)
    for marching in range(STEPS):
        lane_level = jnp.repeat(levels[marching], 2, axis=0)
        drive_volts = port_gain[:, :, None] * lane_level[:, None, :]
        excitation = (drive_volts - resistance[:, :, None] * current - voltage).astype(jnp.bfloat16)

        def near_row(packed):
            index_row, live_count, block_matrix = packed
            selected_blocks = excitation[index_row]
            selected_blocks = jnp.where((entry_index < live_count)[:, None, None], selected_blocks, jnp.zeros((), jnp.bfloat16))
            return jnp.dot(block_matrix.reshape(NEAR * CB, CB).T, selected_blocks.reshape(NEAR * CB, SCENARIOS), preferred_element_type=jnp.float32)

        near_field = lax.map(near_row, (neighbours, live_counts, inductance_near))
        coefficients = jnp.einsum("bkc,bcs->bks", source_basis.astype(jnp.float32), excitation.astype(jnp.float32), precision=lax.Precision.HIGHEST)
        totals = jax.ops.segment_sum(coefficients, member, num_segments=CLUSTERS)
        translated = jnp.dot(translation_wide, totals.reshape(CLUSTERS * RANK, SCENARIOS), precision=lax.Precision.HIGHEST)
        translated = translated.reshape(CLUSTERS, RANK, SCENARIOS)
        chosen = translated[member]
        far_field = jnp.einsum("bkr,bks->brs", target_basis.astype(jnp.float32), chosen, precision=lax.Precision.HIGHEST)
        current = current + near_field + far_field
        voltage = voltage + elastance[:, :, None] * current
    return (current, voltage)
```

```python
import functools

import jax
import jax.numpy as jnp
from jax import lax
from jax.experimental import pallas as pl
from jax.experimental.pallas import tpu as pltpu
from jax.sharding import PartitionSpec as P

MESH = pl.DeviceIdType.MESH
CLUSTERS = 16
RANK = 64
STEPS = 3
BF = jnp.bfloat16
F32 = jnp.float32
WIDE = CLUSTERS * RANK

ONCE = ("a_raw", "a_t", "t_all", "t_sel", "sb", "tb", "tmp", "w_src", "w_tgt", "cols", "wm", "nown", "obuf", "lsem")
EACH = ("ext", "ext_t", "xq", "ns", "nr", "rs", "rr", "zs", "zr", "tot", "ch")
SEMS = ("halo_s", "halo_r", "y_s", "y_r", "n_s", "n_r", "rs_s", "rs_r", "z_s", "z_r", "ag_s", "ag_r", "c_s", "c_r")


def kernel(xn, zn, yn, *refs):
    (cur_in, volt_in, res, ela, port, sym, pick, gate, a_hbm, sb_hbm, tb_hbm, t_hbm, cur, volt) = refs[:14]
    rest = list(refs[14:])
    s = dict(zip(ONCE, rest[: len(ONCE)]))
    rest = rest[len(ONCE):]
    steps = []
    for n in range(STEPS):
        steps.append(dict(zip(EACH, rest[: len(EACH)])))
        rest = rest[len(EACH):]
    sems = dict(zip(SEMS, rest))

    me = lax.axis_index("cells")
    yy = lax.axis_index("cols")
    core = lax.rem(me, 2)
    zz = lax.rem(me // 2, zn)
    xx = me // (2 * zn)
    count = 2 * xn * zn
    chunk = WIDE // xn
    per_x = chunk // 128
    blocks = 8
    pairs = 4
    share = 64

    def cell(x, z, c):
        return (x * zn + z) * 2 + c

    right, left = lax.rem(me + 1, count), lax.rem(me + count - 1, count)
    xc_offsets = [(dx, dc) for dx in range(xn) for dc in range(2) if (dx, dc) != (0, 0)]

    def xc_peer(dx, dc):
        return lax.rem(xx + dx, xn), lax.rem(core + dc, 2)

    def xc_from(dx, dc):
        return lax.rem(xx + xn - dx, xn), lax.rem(core + 2 - dc, 2)

    def y_peer(d):
        return lax.rem(yy + d, yn)

    def y_from(d):
        return lax.rem(yy + yn - d, yn)

    loads = [
        pltpu.make_async_copy(src, dst, s["lsem"].at[i])
        for i, (src, dst) in enumerate(
            ((sb_hbm, s["sb"]), (a_hbm, s["a_raw"]), (t_hbm, s["t_all"]), (tb_hbm, s["tb"]))
        )
    ]
    for load in loads:
        load.start()

    barrier = pltpu.get_barrier_semaphore()
    greeted = [(right, yy), (left, yy)]
    greeted += [(me, y_peer(d)) for d in range(1, yn)]
    for dx, dc in xc_offsets:
        x, c = xc_peer(dx, dc)
        greeted.append((cell(x, zz, c), yy))
    greeted += [(cell(xx, lax.rem(zz + dz, zn), core), yy) for dz in range(1, zn)]
    for device in greeted:
        pl.semaphore_signal(barrier, inc=1, device_id=device, device_id_type=MESH)

    packed = jnp.concatenate(
        [res[...], ela[...], port[...], jnp.zeros((128 - 3 * blocks, 256), F32)], axis=0
    )
    s["tmp"][...] = jnp.transpose(packed)
    s["cols"][...] = s["tmp"][pl.ds(pl.multiple_of(yy * share, share), share), :]

    def column(kind, b):
        at = kind * blocks + b
        return s["cols"][:, at:at + 1]

    cur[...] = cur_in[...]
    volt[...] = volt_in[...]

    def excite(n):
        k = steps[n]
        for p in range(pairs):
            halves = []
            level = (2 * sym[n, p:p + 1, :] - 3).astype(F32) / 3.0
            for b in (2 * p, 2 * p + 1):
                value = column(2, b) * level - column(0, b) * cur[b] - volt[b]
                value = value.astype(BF)
                k["ext"][8 + b] = value
                halves.append(value.astype(F32))
            turned = jnp.transpose(jnp.concatenate(halves, axis=0)).astype(BF)
            for q in range(yn):
                k["ext_t"][q, p] = turned[q * share:(q + 1) * share, :]

    def remote(src, dst, send, recv, device):
        return pltpu.make_async_remote_copy(
            src_ref=src, dst_ref=dst, send_sem=send, recv_sem=recv, device_id=device, device_id_type=MESH
        )

    sent = []

    def send(*args):
        copy = remote(*args)
        copy.start()
        sent.append(copy)

    def arrive(slot, send_sem, recv_sem):
        remote(slot, slot, send_sem, recv_sem, (me, yy)).wait_recv()

    def send_excite(n):
        k = steps[n]
        for d in range(1, yn):
            to = y_peer(d)
            send(k["ext_t"].at[to], k["xq"].at[yy], sems["y_s"].at[n, d], sems["y_r"].at[n, d], (me, to))
        own = k["ext"].at[8:16]
        send(own, k["ext"].at[0:8], sems["halo_s"].at[n, 0], sems["halo_r"].at[n, 0], (right, yy))
        send(own, k["ext"].at[16:24], sems["halo_s"].at[n, 1], sems["halo_r"].at[n, 1], (left, yy))
        k["xq"][yy] = k["ext_t"][yy]

    lane = lax.broadcasted_iota(jnp.int32, (1, 128), 1)
    low_lanes = lane < 64

    def prepare():
        loads[0].wait()
        for p in range(pairs):
            both = jnp.concatenate([s["sb"][2 * p], s["sb"][2 * p + 1]], axis=0).astype(F32)
            turned = jnp.transpose(both)
            for y in range(yn):
                part = turned[y * share:(y + 1) * share, :]
                s["w_src"][p, y * 128:y * 128 + 64, :] = jnp.where(low_lanes, part, 0.0).astype(BF)
                s["w_src"][p, y * 128 + 64:y * 128 + 128, :] = jnp.where(low_lanes, 0.0, part).astype(BF)
        for p in range(pairs):
            for q in range(CLUSTERS // 2):
                def hit(b, g):
                    return gate[b, 16 + g]
                first, second = 2 * p, 2 * p + 1
                at = (p * (CLUSTERS // 2) + q) * 2
                s["wm"][at:at + 1, :] = jnp.where(low_lanes, hit(first, 2 * q), hit(second, 2 * q + 1))
                s["wm"][at + 1:at + 2, :] = jnp.where(low_lanes, hit(second, 2 * q), hit(first, 2 * q + 1))
        loads[1].wait()

        def turn(t, carry):
            for jp in range(8):
                halves = []
                for j in (2 * jp, 2 * jp + 1):
                    halves.append(s["a_raw"][t, j].astype(F32) * gate[t, j])
                both = jnp.concatenate(halves, axis=0)
                s["a_t"][t, :, jp * 128:(jp + 1) * 128] = jnp.transpose(both).astype(BF)
            return carry

        lax.fori_loop(0, blocks, turn, 0)
        loads[2].wait()
        for b in range(blocks):
            s["t_sel"][b * RANK:(b + 1) * RANK, :] = s["t_all"][pick[b, 16]]
        loads[3].wait()
        for p in range(pairs):
            both = jnp.concatenate([s["tb"][2 * p], s["tb"][2 * p + 1]], axis=0).astype(F32)
            s["tmp"][...] = jnp.transpose(both)
            part = s["tmp"][pl.ds(pl.multiple_of(yy * share, share), share), :]
            s["w_tgt"][p, 0:64, :] = jnp.where(low_lanes, part, 0.0).astype(BF)
            s["w_tgt"][p, 64:128, :] = jnp.where(low_lanes, 0.0, part).astype(BF)

    for n in range(STEPS):
        k = steps[n]
        if n == 0:
            excite(0)
            pl.semaphore_wait(barrier, len(greeted))
        send_excite(n)
        if n == 0:
            prepare()
        for d in range(1, yn):
            arrive(k["xq"].at[y_from(d)], sems["y_s"].at[n, d], sems["y_r"].at[n, d])
        straight, rolled = [], []
        for p in range(pairs):
            row = jnp.concatenate([k["xq"][y, p] for y in range(yn)], axis=1)
            c = jnp.dot(row, s["w_src"][p], preferred_element_type=F32)
            straight.append(c)
            rolled.append(pltpu.roll(c, 64, 1))
        for q in range(CLUSTERS // 2):
            total = None
            for p in range(pairs):
                at = (p * (CLUSTERS // 2) + q) * 2
                term = straight[p] * s["wm"][at:at + 1, :] + rolled[p] * s["wm"][at + 1:at + 2, :]
                total = term if total is None else total + term
            xq, lq = q // per_x, q % per_x
            for c in range(2):
                k["rs"][xq, c, :, lq * 128:(lq + 1) * 128] = total[c * 32:(c + 1) * 32, :]
        for e, (dx, dc) in enumerate(xc_offsets):
            x, c = xc_peer(dx, dc)
            send(k["rs"].at[x, c], k["rr"].at[e], sems["rs_s"].at[n, e], sems["rs_r"].at[n, e], (cell(x, zz, c), yy))

        arrive(k["ext"].at[0:8], sems["halo_s"].at[n, 0], sems["halo_r"].at[n, 0])
        arrive(k["ext"].at[16:24], sems["halo_s"].at[n, 1], sems["halo_r"].at[n, 1])

        def near_block(t, carry):
            gathered = jnp.concatenate([k["ext"][pick[t, j]] for j in range(16)], axis=0)
            out = jnp.dot(s["a_t"][t], gathered, preferred_element_type=F32)
            s["obuf"][...] = out
            for y in range(yn):
                k["ns"][y, t] = out[y * share:(y + 1) * share, :].astype(BF)
            s["nown"][t] = s["obuf"][pl.ds(pl.multiple_of(yy * share, share), share), :]
            return carry

        for half in range(2):
            lax.fori_loop(half * 4, half * 4 + 4, near_block, 0)
            part = pl.ds(half * 4, 4)
            for d in range(1, yn):
                to = y_peer(d)
                send(
                    k["ns"].at[to, part],
                    k["nr"].at[d - 1, part],
                    sems["n_s"].at[n, half, d],
                    sems["n_r"].at[n, half, d],
                    (me, to),
                )

        total = k["rs"][xx, core]
        for e in range(len(xc_offsets)):
            arrive(k["rr"].at[e], sems["rs_s"].at[n, e], sems["rs_r"].at[n, e])
            total = total + k["rr"][e]
        k["zs"][...] = total
        for dz in range(1, zn):
            send(
                k["zs"],
                k["zr"].at[dz - 1],
                sems["z_s"].at[n, dz],
                sems["z_r"].at[n, dz],
                (cell(xx, lax.rem(zz + dz, zn), core), yy),
            )
        for dz in range(1, zn):
            arrive(k["zr"].at[dz - 1], sems["z_s"].at[n, dz], sems["z_r"].at[n, dz])
            total = total + k["zr"][dz - 1]

        def rows_of(c):
            return pl.ds(pl.multiple_of(c * 32, 32), 32)

        k["tot"][xx, rows_of(core), :] = total
        own = k["tot"].at[xx, rows_of(core)]
        for e, (dx, dc) in enumerate(xc_offsets):
            x, c = xc_peer(dx, dc)
            send(own, own, sems["ag_s"].at[n, e], sems["ag_r"].at[n, e], (cell(x, zz, c), yy))
        for e, (dx, dc) in enumerate(xc_offsets):
            x, c = xc_from(dx, dc)
            arrive(k["tot"].at[x, rows_of(c)], sems["ag_s"].at[n, e], sems["ag_r"].at[n, e])

        full = jnp.concatenate([k["tot"][x] for x in range(xn)], axis=1)
        high = full.astype(BF)
        low = (full - high.astype(F32)).astype(BF)
        both = lax.dot_general(
            jnp.concatenate([high, low], axis=0),
            s["t_sel"][...],
            (((1,), (1,)), ((), ())),
            preferred_element_type=F32,
        )
        k["ch"][yy] = (both[:64] + both[64:]).astype(BF)
        own = k["ch"].at[yy]
        for d in range(1, yn):
            send(own, own, sems["c_s"].at[n, d], sems["c_r"].at[n, d], (me, y_peer(d)))

        for half in range(2):
            part = pl.ds(half * 4, 4)
            for d in range(1, yn):
                arrive(k["nr"].at[d - 1, part], sems["n_s"].at[n, half, d], sems["n_r"].at[n, half, d])
        for b in range(blocks):
            near = s["nown"][b]
            for d in range(1, yn):
                near = near + k["nr"][d - 1, b].astype(F32)
            cur[b] = cur[b] + near
        for d in range(1, yn):
            arrive(k["ch"].at[y_from(d)], sems["c_s"].at[n, d], sems["c_r"].at[n, d])
        for p in range(pairs):
            picked = jnp.concatenate([k["ch"][y, :, p * 128:(p + 1) * 128] for y in range(yn)], axis=0)
            far = lax.dot_general(
                s["w_tgt"][p], picked, (((1,), (1,)), ((), ())), preferred_element_type=F32
            )
            for i in range(2):
                b = 2 * p + i
                now = cur[b] + far[i * 64:(i + 1) * 64, :]
                cur[b] = now
                volt[b] = volt[b] + column(1, b) * now
        if n + 1 < STEPS:
            excite(n + 1)

    for copy in sent:
        copy.wait_send()


def solution(mesh):
    cells, yn = mesh.shape["cells"], mesh.shape["cols"]
    xn = 4 if cells == 64 else 2
    zn = cells // (2 * xn)
    chunk = WIDE // xn
    peers = 2 * xn - 1
    vmem, dma = pltpu.VMEM, pltpu.SemaphoreType.DMA
    once = [
        vmem((8, 16, 64, 256), BF),
        vmem((8, 256, 1024), BF),
        vmem((CLUSTERS, RANK, WIDE), BF),
        vmem((8 * RANK, WIDE), BF),
        vmem((8, RANK, 256), BF),
        vmem((8, RANK, 256), BF),
        vmem((256, 128), F32),
        vmem((4, 512, 128), BF),
        vmem((4, 128, 128), BF),
        vmem((64, 128), F32),
        vmem((64, 128), F32),
        vmem((8, 64, 256), F32),
        vmem((256, 256), F32),
        dma((4,)),
    ]
    each = [
        vmem((24, 64, 256), BF),
        vmem((yn, 4, 64, 128), BF),
        vmem((yn, 4, 64, 128), BF),
        vmem((yn, 8, 64, 256), BF),
        vmem((yn - 1, 8, 64, 256), BF),
        vmem((xn, 2, 32, chunk), F32),
        vmem((peers, 32, chunk), F32),
        vmem((32, chunk), F32),
        vmem((zn - 1, 32, chunk), F32),
        vmem((xn, 64, chunk), F32),
        vmem((yn, 64, 512), BF),
    ]
    sems = [
        dma((STEPS, 2)),
        dma((STEPS, 2)),
        dma((STEPS, yn)),
        dma((STEPS, yn)),
        dma((STEPS, 2, yn)),
        dma((STEPS, 2, yn)),
        dma((STEPS, peers)),
        dma((STEPS, peers)),
        dma((STEPS, zn)),
        dma((STEPS, zn)),
        dma((STEPS, peers)),
        dma((STEPS, peers)),
        dma((STEPS, yn)),
        dma((STEPS, yn)),
    ]
    in_vmem = pl.BlockSpec(memory_space=pltpu.VMEM)
    in_smem = pl.BlockSpec(memory_space=pltpu.SMEM)
    anywhere = pl.BlockSpec(memory_space=pl.ANY)

    def per_device(
        current, voltage, resistance, elastance, port_gain, symbols, neighbours, live_counts, membership, near, sb, tb, trans
    ):
        entry = lax.broadcasted_iota(jnp.int32, (8, 32), 1)
        gate = jnp.where(entry < 16, entry < live_counts[:, None], entry - 16 == membership).astype(F32)
        anchor = lax.axis_index("cells") * 8 - 8
        pick = jnp.concatenate([neighbours - anchor, membership], axis=1)
        args = (
            current, voltage, resistance, elastance, port_gain, symbols, pick, gate, near, sb, tb,
            trans.reshape(CLUSTERS, RANK, WIDE),
        )
        state = jax.ShapeDtypeStruct(current.shape, F32)
        return pl.pallas_call(
            functools.partial(kernel, xn, zn, yn),
            out_shape=(state, state),
            in_specs=[in_vmem] * 6 + [in_smem] * 2 + [anywhere] * 4,
            out_specs=(in_vmem, in_vmem),
            scratch_shapes=once + each * STEPS + sems,
            compiler_params=pltpu.CompilerParams(
                collective_id=0, has_side_effects=True, vmem_limit_bytes=60 * 1024 * 1024
            ),
        )(*args)

    placed = (
        P("cells", "cols", None),
        P("cells", "cols", None),
        P("cells", None),
        P("cells", None),
        P("cells", None),
        P(None, "cells", None),
        P("cells", None),
        P("cells"),
        P("cells", None),
        P("cells", None, "cols", None),
        P("cells", None, None),
        P("cells", None, None),
        P(),
    )
    return jax.shard_map(
        per_device,
        mesh=mesh,
        in_specs=placed,
        out_specs=(P("cells", "cols", None), P("cells", "cols", None)),
        check_vma=False,
    )
```

```python
import functools

import jax
import jax.numpy as jnp
from jax import lax
from jax.experimental import pallas as pl
from jax.experimental.pallas import tpu as pltpu
from jax.sharding import PartitionSpec as P

MESH = pl.DeviceIdType.MESH
CLUSTERS = 16
RANK = 64
STEPS = 3
PIECES = 2
BF = jnp.bfloat16
F32 = jnp.float32
WIDE = CLUSTERS * RANK

ONCE = ("a_raw", "a_t", "t_all", "t_sel", "sb", "tb", "tmp", "w_src", "w_tgt", "cols", "wm", "nown", "obuf", "lsem")
EACH = ("ext", "ext_t", "xq", "ns", "nr", "rs", "rr", "zs", "zr", "tot", "ch")
SEMS = ("halo_s", "halo_r", "y_s", "y_r", "n_s", "n_r", "rs_s", "rs_r", "z_s", "z_r", "ag_s", "ag_r", "c_s", "c_r")


def kernel(xn, zn, yn, *refs):
    (cur_in, volt_in, res, ela, port, sym, pick, a_hbm, sb_hbm, tb_hbm, t_hbm, cur, volt, last) = refs[:14]
    rest = list(refs[14:])
    s = dict(zip(ONCE, rest[: len(ONCE)]))
    rest = rest[len(ONCE):]
    steps = []
    for n in range(STEPS):
        steps.append(dict(zip(EACH, rest[: len(EACH)])))
        rest = rest[len(EACH):]
    sems = dict(zip(SEMS, rest))

    me = lax.axis_index("cells")
    yy = lax.axis_index("cols")
    core = lax.rem(me, 2)
    zz = lax.rem(me // 2, zn)
    xx = me // (2 * zn)
    count = 2 * xn * zn
    chunk = WIDE // xn
    per_x = chunk // 128
    blocks = 8
    pairs = 4
    share = 64
    piece = share // PIECES
    sub = piece // 2

    def cell(x, z, c):
        return (x * zn + z) * 2 + c

    right, left = lax.rem(me + 1, count), lax.rem(me + count - 1, count)
    xc_offsets = [(dx, dc) for dx in range(xn) for dc in range(2) if (dx, dc) != (0, 0)]

    def xc_peer(dx, dc):
        return lax.rem(xx + dx, xn), lax.rem(core + dc, 2)

    def xc_from(dx, dc):
        return lax.rem(xx + xn - dx, xn), lax.rem(core + 2 - dc, 2)

    def y_peer(d):
        return lax.rem(yy + d, yn)

    def y_from(d):
        return lax.rem(yy + yn - d, yn)

    loads = [
        pltpu.make_async_copy(src, dst, s["lsem"].at[i])
        for i, (src, dst) in enumerate(
            ((sb_hbm, s["sb"]), (a_hbm, s["a_raw"]), (t_hbm, s["t_all"]), (tb_hbm, s["tb"]), (cur_in, cur), (volt_in, volt))
        )
    ]
    for i in (4, 5, 0, 1, 2, 3):
        loads[i].start()

    barrier = pltpu.get_barrier_semaphore()
    greeted = [(right, yy), (left, yy)]
    greeted += [(me, y_peer(d)) for d in range(1, yn)]
    for dx, dc in xc_offsets:
        x, c = xc_peer(dx, dc)
        greeted.append((cell(x, zz, c), yy))
    greeted += [(cell(xx, lax.rem(zz + dz, zn), core), yy) for dz in range(1, zn)]
    for device in greeted:
        pl.semaphore_signal(barrier, inc=1, device_id=device, device_id_type=MESH)

    packed = jnp.concatenate(
        [res[...], ela[...], port[...], jnp.zeros((128 - 3 * blocks, 256), F32)], axis=0
    )
    s["tmp"][...] = jnp.transpose(packed)
    s["cols"][...] = s["tmp"][pl.ds(pl.multiple_of(yy * share, share), share), :]

    def column(kind, b):
        at = kind * blocks + b
        return s["cols"][:, at:at + 1]

    def excite(n):
        k = steps[n]
        for p in range(pairs):
            halves = []
            level = (2 * sym[n, p:p + 1, :] - 3).astype(F32) / 3.0
            for b in (2 * p, 2 * p + 1):
                value = column(2, b) * level - column(0, b) * cur[b] - volt[b]
                value = value.astype(BF)
                k["ext"][8 + b] = value
                halves.append(value.astype(F32))
            turned = jnp.transpose(jnp.concatenate(halves, axis=0)).astype(BF)
            for q in range(yn):
                for h in range(PIECES):
                    at = q * share + h * piece
                    k["ext_t"][q, h, p] = turned[at:at + piece, :]

    def remote(src, dst, send, recv, device):
        return pltpu.make_async_remote_copy(
            src_ref=src, dst_ref=dst, send_sem=send, recv_sem=recv, device_id=device, device_id_type=MESH
        )

    sent = []

    def send(*args):
        copy = remote(*args)
        copy.start()
        sent.append(copy)

    def arrive(slot, send_sem, recv_sem):
        remote(slot, slot, send_sem, recv_sem, (me, yy)).wait_recv()

    def send_excite(n):
        k = steps[n]
        for h in range(PIECES):
            for d in range(1, yn):
                to = y_peer(d)
                send(
                    k["ext_t"].at[to, h], k["xq"].at[yy, h], sems["y_s"].at[n, h, d], sems["y_r"].at[n, h, d], (me, to)
                )
        own = k["ext"].at[8:16]
        send(own, k["ext"].at[0:8], sems["halo_s"].at[n, 0], sems["halo_r"].at[n, 0], (right, yy))
        send(own, k["ext"].at[16:24], sems["halo_s"].at[n, 1], sems["halo_r"].at[n, 1], (left, yy))
        k["xq"][yy] = k["ext_t"][yy]

    lane = lax.broadcasted_iota(jnp.int32, (1, 128), 1)
    low_lanes = lane < 64

    def prepare():
        loads[0].wait()
        for p in range(pairs):
            both = jnp.concatenate([s["sb"][2 * p], s["sb"][2 * p + 1]], axis=0).astype(F32)
            turned = jnp.transpose(both)
            for y in range(yn):
                part = turned[y * share:(y + 1) * share, :]
                s["w_src"][p, y * 128:y * 128 + 64, :] = jnp.where(low_lanes, part, 0.0).astype(BF)
                s["w_src"][p, y * 128 + 64:y * 128 + 128, :] = jnp.where(low_lanes, 0.0, part).astype(BF)
        for p in range(pairs):
            for q in range(CLUSTERS // 2):
                def hit(b, g):
                    return pick[b, 32 + g].astype(F32)
                first, second = 2 * p, 2 * p + 1
                at = (p * (CLUSTERS // 2) + q) * 2
                s["wm"][at:at + 1, :] = jnp.where(low_lanes, hit(first, 2 * q), hit(second, 2 * q + 1))
                s["wm"][at + 1:at + 2, :] = jnp.where(low_lanes, hit(second, 2 * q), hit(first, 2 * q + 1))
        loads[1].wait()

        def turn(t, carry):
            for jp in range(8):
                halves = []
                for j in (2 * jp, 2 * jp + 1):
                    halves.append(s["a_raw"][t, j].astype(F32) * pick[t, 16 + j].astype(F32))
                both = jnp.concatenate(halves, axis=0)
                s["a_t"][t, :, jp * 128:(jp + 1) * 128] = jnp.transpose(both).astype(BF)
            return carry

        lax.fori_loop(0, blocks, turn, 0)
        loads[2].wait()
        for b in range(blocks):
            s["t_sel"][b * RANK:(b + 1) * RANK, :] = s["t_all"][pick[b, 48]]
        loads[3].wait()
        for p in range(pairs):
            both = jnp.concatenate([s["tb"][2 * p], s["tb"][2 * p + 1]], axis=0).astype(F32)
            s["tmp"][...] = jnp.transpose(both)
            part = s["tmp"][pl.ds(pl.multiple_of(yy * share, share), share), :]
            s["w_tgt"][p, 0:64, :] = jnp.where(low_lanes, part, 0.0).astype(BF)
            s["w_tgt"][p, 64:128, :] = jnp.where(low_lanes, 0.0, part).astype(BF)

    for n in range(STEPS):
        k = steps[n]
        if n == 0:
            loads[4].wait()
            loads[5].wait()
            excite(0)
            pl.semaphore_wait(barrier, len(greeted))
        send_excite(n)
        if n == 0:
            prepare()
        for h in range(PIECES):
            for d in range(1, yn):
                arrive(k["xq"].at[y_from(d), h], sems["y_s"].at[n, h, d], sems["y_r"].at[n, h, d])
            straight, rolled = [], []
            for p in range(pairs):
                row = jnp.concatenate([k["xq"][y, h, p] for y in range(yn)], axis=1)
                c = jnp.dot(row, s["w_src"][p], preferred_element_type=F32)
                straight.append(c)
                rolled.append(pltpu.roll(c, 64, 1))
            for q in range(CLUSTERS // 2):
                total = None
                for p in range(pairs):
                    at = (p * (CLUSTERS // 2) + q) * 2
                    term = straight[p] * s["wm"][at:at + 1, :] + rolled[p] * s["wm"][at + 1:at + 2, :]
                    total = term if total is None else total + term
                xq, lq = q // per_x, q % per_x
                for c in range(2):
                    k["rs"][h, xq, c, :, lq * 128:(lq + 1) * 128] = total[c * sub:(c + 1) * sub, :]
            for e, (dx, dc) in enumerate(xc_offsets):
                x, c = xc_peer(dx, dc)
                send(
                    k["rs"].at[h, x, c],
                    k["rr"].at[h, e],
                    sems["rs_s"].at[n, h, e],
                    sems["rs_r"].at[n, h, e],
                    (cell(x, zz, c), yy),
                )

        arrive(k["ext"].at[0:8], sems["halo_s"].at[n, 0], sems["halo_r"].at[n, 0])
        arrive(k["ext"].at[16:24], sems["halo_s"].at[n, 1], sems["halo_r"].at[n, 1])

        def near_block(t, carry):
            gathered = jnp.concatenate([k["ext"][pick[t, j]] for j in range(16)], axis=0)
            out = jnp.dot(s["a_t"][t], gathered, preferred_element_type=F32)
            s["obuf"][...] = out
            for y in range(yn):
                k["ns"][y, t] = out[y * share:(y + 1) * share, :].astype(BF)
            s["nown"][t] = s["obuf"][pl.ds(pl.multiple_of(yy * share, share), share), :]
            return carry

        def near_half(half):
            lax.fori_loop(half * 4, half * 4 + 4, near_block, 0)
            part = pl.ds(half * 4, 4)
            for d in range(1, yn):
                to = y_peer(d)
                send(
                    k["ns"].at[to, part],
                    k["nr"].at[d - 1, part],
                    sems["n_s"].at[n, half, d],
                    sems["n_r"].at[n, half, d],
                    (me, to),
                )

        near_half(0)

        for h in range(PIECES):
            total = k["rs"][h, xx, core]
            for e in range(len(xc_offsets)):
                arrive(k["rr"].at[h, e], sems["rs_s"].at[n, h, e], sems["rs_r"].at[n, h, e])
                total = total + k["rr"][h, e]
            k["zs"][h] = total
            for dz in range(1, zn):
                send(
                    k["zs"].at[h],
                    k["zr"].at[h, dz - 1],
                    sems["z_s"].at[n, h, dz],
                    sems["z_r"].at[n, h, dz],
                    (cell(xx, lax.rem(zz + dz, zn), core), yy),
                )

        near_half(1)

        for h in range(PIECES):
            total = k["zs"][h]
            for dz in range(1, zn):
                arrive(k["zr"].at[h, dz - 1], sems["z_s"].at[n, h, dz], sems["z_r"].at[n, h, dz])
                total = total + k["zr"][h, dz - 1]
            k["tot"][h, xx, core] = total
            own = k["tot"].at[h, xx, core]
            for e, (dx, dc) in enumerate(xc_offsets):
                x, c = xc_peer(dx, dc)
                send(own, own, sems["ag_s"].at[n, h, e], sems["ag_r"].at[n, h, e], (cell(x, zz, c), yy))

        for h in range(PIECES):
            for e, (dx, dc) in enumerate(xc_offsets):
                x, c = xc_from(dx, dc)
                arrive(k["tot"].at[h, x, c], sems["ag_s"].at[n, h, e], sems["ag_r"].at[n, h, e])
            full = jnp.concatenate(
                [jnp.concatenate([k["tot"][h, x, 0], k["tot"][h, x, 1]], axis=0) for x in range(xn)], axis=1
            )
            high = full.astype(BF)
            low = (full - high.astype(F32)).astype(BF)
            both = lax.dot_general(
                jnp.concatenate([high, low], axis=0),
                s["t_sel"][...],
                (((1,), (1,)), ((), ())),
                preferred_element_type=F32,
            )
            k["ch"][yy, h] = (both[:piece] + both[piece:]).astype(BF)
            own = k["ch"].at[yy, h]
            for d in range(1, yn):
                send(own, own, sems["c_s"].at[n, h, d], sems["c_r"].at[n, h, d], (me, y_peer(d)))

        for half in range(2):
            part = pl.ds(half * 4, 4)
            for d in range(1, yn):
                arrive(k["nr"].at[d - 1, part], sems["n_s"].at[n, half, d], sems["n_r"].at[n, half, d])
        for b in range(blocks):
            near = s["nown"][b]
            for d in range(1, yn):
                near = near + k["nr"][d - 1, b].astype(F32)
            cur[b] = cur[b] + near
        for h in range(PIECES):
            for d in range(1, yn):
                arrive(k["ch"].at[y_from(d), h], sems["c_s"].at[n, h, d], sems["c_r"].at[n, h, d])
        for p in range(pairs):
            picked = jnp.concatenate([k["ch"][y, h, :, p * 128:(p + 1) * 128] for y in range(yn) for h in range(PIECES)], axis=0)
            far = lax.dot_general(
                s["w_tgt"][p], picked, (((1,), (1,)), ((), ())), preferred_element_type=F32
            )
            for i in range(2):
                b = 2 * p + i
                if n + 1 == STEPS:
                    last[b] = far[i * 64:(i + 1) * 64, :]
                    continue
                now = cur[b] + far[i * 64:(i + 1) * 64, :]
                cur[b] = now
                volt[b] = volt[b] + column(1, b) * now
        if n + 1 < STEPS:
            excite(n + 1)

    for copy in sent:
        copy.wait_send()


def solution(mesh):
    cells, yn = mesh.shape["cells"], mesh.shape["cols"]
    xn = 4 if cells == 64 else 2
    zn = cells // (2 * xn)
    chunk = WIDE // xn
    piece = 64 // PIECES
    peers = 2 * xn - 1
    vmem, dma = pltpu.VMEM, pltpu.SemaphoreType.DMA
    once = [
        vmem((8, 16, 64, 256), BF),
        vmem((8, 256, 1024), BF),
        vmem((CLUSTERS, RANK, WIDE), BF),
        vmem((8 * RANK, WIDE), BF),
        vmem((8, RANK, 256), BF),
        vmem((8, RANK, 256), BF),
        vmem((256, 128), F32),
        vmem((4, 512, 128), BF),
        vmem((4, 128, 128), BF),
        vmem((64, 128), F32),
        vmem((64, 128), F32),
        vmem((8, 64, 256), F32),
        vmem((256, 256), F32),
        dma((6,)),
    ]
    each = [
        vmem((24, 64, 256), BF),
        vmem((yn, PIECES, 4, piece, 128), BF),
        vmem((yn, PIECES, 4, piece, 128), BF),
        vmem((yn, 8, 64, 256), BF),
        vmem((yn - 1, 8, 64, 256), BF),
        vmem((PIECES, xn, 2, piece // 2, chunk), F32),
        vmem((PIECES, peers, piece // 2, chunk), F32),
        vmem((PIECES, piece // 2, chunk), F32),
        vmem((PIECES, zn - 1, piece // 2, chunk), F32),
        vmem((PIECES, xn, 2, piece // 2, chunk), F32),
        vmem((yn, PIECES, piece, 512), BF),
    ]
    sems = [
        dma((STEPS, 2)),
        dma((STEPS, 2)),
        dma((STEPS, PIECES, yn)),
        dma((STEPS, PIECES, yn)),
        dma((STEPS, 2, yn)),
        dma((STEPS, 2, yn)),
        dma((STEPS, PIECES, peers)),
        dma((STEPS, PIECES, peers)),
        dma((STEPS, PIECES, zn)),
        dma((STEPS, PIECES, zn)),
        dma((STEPS, PIECES, peers)),
        dma((STEPS, PIECES, peers)),
        dma((STEPS, PIECES, yn)),
        dma((STEPS, PIECES, yn)),
    ]
    in_vmem = pl.BlockSpec(memory_space=pltpu.VMEM)
    in_smem = pl.BlockSpec(memory_space=pltpu.SMEM)
    anywhere = pl.BlockSpec(memory_space=pl.ANY)

    def per_device(
        current, voltage, resistance, elastance, port_gain, symbols, neighbours, live_counts, membership, near, sb, tb, trans
    ):
        at = lax.broadcasted_iota(jnp.int32, (8, 64), 1)
        local = jnp.pad(neighbours, ((0, 0), (0, 48))) - (lax.axis_index("cells") * 8 - 8)
        used = (at - 16 < live_counts[:, None]).astype(jnp.int32)
        inside = (at - 32 == membership).astype(jnp.int32)
        pick = jnp.where(at < 16, local, jnp.where(at < 32, used, jnp.where(at < 48, inside, membership)))
        args = (
            current, voltage, resistance, elastance, port_gain, symbols, pick, near, sb, tb,
            trans.reshape(CLUSTERS, RANK, WIDE),
        )
        state = jax.ShapeDtypeStruct(current.shape, F32)
        partial, before, far = pl.pallas_call(
            functools.partial(kernel, xn, zn, yn),
            out_shape=(state, state, state),
            in_specs=[anywhere] * 2 + [in_vmem] * 4 + [in_smem] + [anywhere] * 4,
            out_specs=(in_vmem, in_vmem, in_vmem),
            scratch_shapes=once + each * STEPS + sems,
            compiler_params=pltpu.CompilerParams(
                collective_id=0, has_side_effects=True, vmem_limit_bytes=60 * 1024 * 1024
            ),
        )(*args)
        rows = lax.dynamic_slice_in_dim(elastance, lax.axis_index("cols") * 64, 64, 1)
        after = partial + far
        return after, before + rows[:, :, None] * after

    placed = (
        P("cells", "cols", None),
        P("cells", "cols", None),
        P("cells", None),
        P("cells", None),
        P("cells", None),
        P(None, "cells", None),
        P("cells", None),
        P("cells"),
        P("cells", None),
        P("cells", None, "cols", None),
        P("cells", None, None),
        P("cells", None, None),
        P(),
    )
    return jax.shard_map(
        per_device,
        mesh=mesh,
        in_specs=placed,
        out_specs=(P("cells", "cols", None), P("cells", "cols", None)),
        check_vma=False,
    )
```
